32 devices in a mesh: sub: 4 (over z), blk: 8 (over y, x, core).
Axes of the slice: x: 2, y: 2, z: 4, core: 2. Of those that a mesh axis runs over, the one named last changes fastest.
Arguments:
- mode_blocks: float32 [36864, 1024], P(('sub', 'blk')), may hold values from -6 to 6
- stiffness: bfloat16 [8192, 5760], P(('sub', 'blk')), may hold values from -0.078125 to 0.078125
- mass_tiles: bfloat16 [8192, 5760], P(('sub', 'blk')), may hold values from -0.078125 to 0.078125
- reader_ids: int32 [32, 5], P(('sub', 'blk')), may hold values from 0 to 31, as said below
- owner_slot: int32 [32], replicated, may hold values from 0 to 31, as said below
- tile_mask: int32 [64, 45], P(('sub', 'blk')), may hold values 0 or 1
- tree_order: int32 [8192], P(('sub', 'blk')), may hold values from 0 to 255, as said below
Outputs:
- stiff_tree: bfloat16 [8192, 1024], P(('sub', 'blk'))
- mass_tree: bfloat16 [8192, 1024], P(('sub', 'blk'))
The draws below stay inside these ranges and needn't reach their ends.
Inputs may be any that keep to these rules, and one draw needn't show every extreme that they name: A permutation: interface i is held at slot owner_slot[i]. `reader_ids`: the 5 interfaces of a row block are distinct, include the one held at its own slot, and are held at slots no more than 4 away from its own index. `tree_order`: within each row block a permutation of 0 to 255.
All inputs are finite; a program needn't handle non-finite values. No bound on the sum of `tile_mask` on one device may be relied on, other than what follows from the above.
Results may differ from the reference program's by a relative error of at most 0.001.
Values may be sent and summed in bfloat16 or wider, within the bound.
No kernel may reach another device: no remote copies, remote signals or barrier semaphores. Data moves between devices by JAX's collectives and lax.ppermute only.
A program may use at most 192 MiB of HBM per device.

```python
import jax
import jax.numpy as jnp
from jax import lax

MODES = 1024
TILE = 128
IFACE_DOF = 1152
ROWS = 256
REACH = 4
READS = 5
IFACES = 32
TOTROWS = 8192
N_SUB = 4
N_BLK = 8


def layout_slots(key):
    return jax.random.permutation(jax.random.fold_in(key, 11), IFACES).astype(jnp.int32)


def draw_owner_slot(key, part):
    return layout_slots(key)


def draw_reader_ids(key, part):
    owner = layout_slots(key)
    inverse = jnp.argsort(owner).astype(jnp.int32)
    span = 2 * REACH + 1
    offsets = jnp.arange(span, dtype=jnp.int32) - REACH
    devices_col = jnp.arange(IFACES, dtype=jnp.int32)[:, None]
    slot_grid = devices_col + offsets[None, :]
    valid = (slot_grid >= 0) & (slot_grid < IFACES)
    scores = jax.random.randint(jax.random.fold_in(key, 23), (IFACES, span), 0, 1 << 20) * span + jnp.arange(span, dtype=jnp.int32)[None, :]
    scores = jnp.where(valid, scores, 1 << 30)
    scores = jnp.where(offsets[None, :] == 0, -1, scores)
    chosen = jnp.argsort(scores, axis=1)[:, :READS].astype(jnp.int32)
    mixing = jax.random.randint(jax.random.fold_in(key, 37), (IFACES, READS), 0, 1 << 20) * READS + jnp.arange(READS, dtype=jnp.int32)[None, :]
    shuffle = jnp.argsort(mixing, axis=1)
    chosen = jnp.take_along_axis(chosen, shuffle, axis=1)
    slot_read = devices_col + chosen - REACH
    return inverse[slot_read].astype(jnp.int32)


def draw_tree_order(key, part):
    keys = jax.random.split(jax.random.fold_in(key, 53), IFACES)
    orders = jax.vmap(lambda single: jax.random.permutation(single, ROWS))(keys)
    return orders.reshape(-1).astype(jnp.int32)


def touch_ends(entries, stream_key, low, top_value):
    index_at = [jax.random.randint(jax.random.fold_in(stream_key, axis), (), 0, length) for axis, length in enumerate(entries.shape)]
    longest = entries.shape.index(max(entries.shape))
    next_to = index_at[:longest] + [(index_at[longest] + 1) % entries.shape[longest]] + index_at[longest + 1:]
    return entries.at[tuple(index_at)].set(low).at[tuple(next_to)].set(top_value)


def shard_levels(key, dims, shards, low, top_value):
    def one(dim, blocks):
        steps = jax.random.uniform(jax.random.fold_in(jax.random.fold_in(key, 6), dim), (blocks,), jnp.float32, low / len(shards), top_value / len(shards))
        return jnp.repeat(jnp.exp(steps), dims[dim] // blocks).reshape((-1,) + (1,) * (len(dims) - dim - 1))

    loudness = one(*shards[0])
    for cut in shards[1:]:
        loudness = loudness * one(*cut)
    return loudness


def normal_values(key, shape, scale, reach, pieces=(), held_as=jnp.bfloat16):
    level = shard_levels(key, shape, pieces, -0.22, 0.18) if pieces else 1.0
    drawn = jax.random.normal(key, shape, jnp.float32) * scale * level
    return jnp.minimum(jnp.maximum(drawn, -reach), reach).astype(held_as)


def setup_inputs(seed: int = 0) -> dict:
    splits = jax.random.split(jax.random.key(seed), 8)
    return {
        "mode_blocks": normal_values(splits[0], (IFACES * IFACE_DOF, MODES), 1.0, 6.0, ((0, 32),), jnp.float32),
        "stiffness": normal_values(splits[1], (TOTROWS, READS * IFACE_DOF), (READS * IFACE_DOF) ** -0.5, 0.078125, ((0, 32),)),
        "mass_tiles": normal_values(splits[2], (TOTROWS, READS * IFACE_DOF), (READS * IFACE_DOF) ** -0.5, 0.078125, ((0, 32),)),
        "reader_ids": draw_reader_ids(jax.random.fold_in(splits[7], 71), 0),
        "owner_slot": draw_owner_slot(jax.random.fold_in(splits[7], 71), 0),
        "tile_mask": touch_ends((jax.random.randint(splits[5], (TOTROWS // TILE, READS * IFACE_DOF // TILE), 0, 4) < 3).astype(jnp.int32), jax.random.fold_in(splits[5], 1), 0, 1),
        "tree_order": draw_tree_order(jax.random.fold_in(splits[7], 71), 0),
    }


def masked_tiles(block, mask):
    shaped = block.astype(jnp.float32).reshape(mask.shape[0], TILE, mask.shape[1], TILE)
    return (shaped * mask.astype(jnp.float32)[:, None, :, None]).reshape(block.shape)


def reference(mode_blocks, stiffness, mass_tiles, reader_ids, owner_slot, tile_mask, tree_order):
    blocks = N_SUB * N_BLK
    tiles = ROWS // TILE
    tile_cols = READS * IFACE_DOF // TILE
    phi_all = mode_blocks.reshape(blocks, IFACE_DOF, MODES)
    slots = owner_slot[reader_ids]

    def project(item):
        stiff_rows, mass_rows, slot_row, mask_rows = item
        picked = phi_all[slot_row].reshape(READS * IFACE_DOF, MODES)
        stiff_out = jnp.dot(masked_tiles(stiff_rows, mask_rows), picked, precision=lax.Precision.HIGHEST, preferred_element_type=jnp.float32)
        mass_out = jnp.dot(masked_tiles(mass_rows, mask_rows), picked, precision=lax.Precision.HIGHEST, preferred_element_type=jnp.float32)
        return stiff_out.astype(jnp.bfloat16), mass_out.astype(jnp.bfloat16)

    stiff_proj, mass_proj = lax.map(project, (stiffness.reshape(blocks, ROWS, READS * IFACE_DOF), mass_tiles.reshape(blocks, ROWS, READS * IFACE_DOF), slots, tile_mask.reshape(blocks, tiles, tile_cols)))
    piece_rows = ROWS // N_BLK
    order = tree_order.reshape(blocks, ROWS, 1)

    def relay(values):
        values = values.reshape(N_SUB, N_BLK, N_BLK, piece_rows, MODES).transpose(0, 2, 1, 3, 4).reshape(blocks, ROWS, MODES)
        return jnp.take_along_axis(values, order, axis=1).reshape(blocks * ROWS, MODES)

    return relay(stiff_proj), relay(mass_proj)
```

```python
import functools

import jax
import jax.numpy as jnp
from jax import lax
from jax.experimental import pallas as pl
from jax.experimental.pallas import tpu as pltpu
from jax.sharding import PartitionSpec as P

TILE = 128
REACH = 4
AXES = ("sub", "blk")
STEPS = 64.0
TOP = 32760.0
CODE_ROWS = 16


def quantize(x_ref, q_ref):
    tiles = x_ref.shape[0] // TILE
    codes = []
    for t in range(tiles):
        rows = pl.ds(t * TILE, TILE)
        x = x_ref[rows, :]
        top = jnp.maximum(jnp.max(jnp.abs(x), axis=0, keepdims=True), 2.0**-120)
        code = jnp.ceil(jnp.log2(top) * STEPS + 0.5)
        q = x * (jnp.exp2(code * (-1.0 / STEPS)) * TOP)
        q = jnp.minimum(jnp.maximum(q, -32767.0), 32767.0)
        q_ref[rows, :] = jnp.round(q).astype(jnp.int32).astype(jnp.int16)
        codes.append(code.astype(jnp.int32))
    codes.append(jnp.zeros((CODE_ROWS - tiles, x_ref.shape[1]), jnp.int32))
    q_ref[pl.ds(tiles * TILE, CODE_ROWS), :] = jnp.concatenate(codes, axis=0).astype(jnp.int16)


def pack_kernel(place_ref, keep_in, send_in, keep_ref, send_ref):
    quantize(keep_in, keep_ref)
    quantize(send_in, send_ref)


def pack(place, mode_blocks, width):
    rows, modes = mode_blocks.shape
    half = modes // 2
    per_half = half // width
    out = jax.ShapeDtypeStruct((rows + CODE_ROWS, half), jnp.int16)
    return pl.pallas_call(
        pack_kernel,
        grid_spec=pltpu.PrefetchScalarGridSpec(
            num_scalar_prefetch=1,
            grid=(per_half,),
            in_specs=[
                pl.BlockSpec((rows, width), lambda i, place: (0, (place[0] % 2) * per_half + i)),
                pl.BlockSpec((rows, width), lambda i, place: (0, (1 - place[0] % 2) * per_half + i)),
            ],
            out_specs=[pl.BlockSpec((rows + CODE_ROWS, width), lambda i, place: (0, i))] * 2,
        ),
        out_shape=(out, out),
        compiler_params=pltpu.CompilerParams(vmem_limit_bytes=32 << 20),
        name="pack",
    )(place, mode_blocks, mode_blocks)


def project_kernel(reads, pieces, place_ref, owner_ref, *refs):
    ids, masks = refs[0:2], refs[2:4]
    stiff, mass = refs[4:6], refs[6:8]
    held = refs[8 : 8 + pieces]
    out_ref, total, left, high, low = refs[8 + pieces :]
    read = pl.program_id(0)
    core = place_ref[0] % 2
    first = place_ref[0] - core - REACH
    rows = stiff[0].shape[0]
    depth = high.shape[0]
    tiles = depth // TILE

    @pl.when(read == 0)
    def _():
        total[...] = jnp.zeros_like(total)

    for who in range(2):
        offset = owner_ref[ids[who][0, read]] - first
        piece = (offset // 2) * 2 + (offset % 2 + core) % 2
        for k in range(pieces):

            @pl.when(piece == k)
            def _(k=k):
                codes = held[k][pl.ds(depth, CODE_ROWS), :].astype(jnp.int32).astype(jnp.float32)
                scale = jnp.exp2(codes * (1.0 / STEPS)) * (1.0 / TOP)
                for t in range(tiles):
                    span = pl.ds(t * TILE, TILE)
                    value = held[k][span, :].astype(jnp.int32).astype(jnp.float32) * scale[t : t + 1, :]
                    top = value.astype(jnp.bfloat16)
                    high[span, :] = top
                    low[span, :] = (value - top.astype(jnp.float32)).astype(jnp.bfloat16)

        for kind, source in enumerate((stiff[who], mass[who])):
            for r in range(rows // TILE):
                for t in range(tiles):
                    keep = masks[who][r, read * tiles + t] != 0
                    tile = source[pl.ds(r * TILE, TILE), pl.ds(t * TILE, TILE)]
                    left[pl.ds(kind * rows + r * TILE, TILE), pl.ds(t * TILE, TILE)] = jnp.where(keep, tile, jnp.zeros_like(tile))
        total[who] += jnp.dot(left[...], high[...], preferred_element_type=jnp.float32) + jnp.dot(
            left[...], low[...], preferred_element_type=jnp.float32
        )

    @pl.when(read == reads - 1)
    def _():
        devices, _, _, part, _ = out_ref.shape
        for who in range(2):
            for kind in range(2):
                for j in range(devices):
                    out_ref[j, who, kind] = total[who, pl.ds(kind * rows + j * part, part), :].astype(jnp.bfloat16)


def project(place, owner_slot, ids, masks, stiff, mass, held, devices):
    rows, reads = stiff[0].shape[0], ids[0].shape[1]
    depth = stiff[0].shape[1] // reads
    width = held[0].shape[1]
    whole = pl.BlockSpec(held[0].shape, lambda r, *_: (0, 0), pipeline_mode=pl.Buffered(1))
    part = rows // devices
    return pl.pallas_call(
        functools.partial(project_kernel, reads, len(held)),
        grid_spec=pltpu.PrefetchScalarGridSpec(
            num_scalar_prefetch=6,
            grid=(reads,),
            in_specs=[pl.BlockSpec((rows, depth), lambda r, *_: (0, r))] * 4 + [whole] * len(held),
            out_specs=pl.BlockSpec((devices, 2, 2, part, width), lambda r, *_: (0, 0, 0, 0, 0)),
            scratch_shapes=[
                pltpu.VMEM((2, 2 * rows, width), jnp.float32),
                pltpu.VMEM((2 * rows, depth), jnp.bfloat16),
                pltpu.VMEM((depth, width), jnp.bfloat16),
                pltpu.VMEM((depth, width), jnp.bfloat16),
            ],
        ),
        out_shape=jax.ShapeDtypeStruct((devices, 2, 2, part, width), jnp.bfloat16),
        compiler_params=pltpu.CompilerParams(vmem_limit_bytes=48 << 20),
        cost_estimate=pl.CostEstimate(
            flops=2 * 2 * 2 * 2 * rows * depth * reads * width,
            bytes_accessed=4 * rows * depth * reads * 2 + len(held) * depth * width * 2,
            transcendentals=0,
        ),
        name="project",
    )(place, owner_slot, *ids, *masks, *stiff, *mass, *held)


def order_kernel(order_ref, rows_ref, stiff_ref, mass_ref):
    source = pl.program_id(0)
    chips, _, _, _, part, width = rows_ref.shape
    count = order_ref.shape[0]
    at = lax.broadcasted_iota(jnp.int32, (count, chips * 2 * part), 1)
    block = at // part
    owner = (block // 2) * 2 + (block % 2 + source) % 2
    pick = (order_ref[...] == owner * part + at % part).astype(jnp.bfloat16)
    for kind, ref in enumerate((stiff_ref, mass_ref)):
        rows = rows_ref[:, 0, :, kind]
        if part % 16:
            rows = rows.astype(jnp.float32).reshape(count, width).astype(jnp.bfloat16)
        else:
            rows = rows.reshape(count, width)
        ref[...] = jnp.dot(pick, rows, preferred_element_type=jnp.float32).astype(jnp.bfloat16)


def order_rows(tree_order, rows):
    chips, _, _, _, part, width = rows.shape
    count = tree_order.shape[0]
    out = jax.ShapeDtypeStruct((count, 2 * width), jnp.bfloat16)
    return pl.pallas_call(
        order_kernel,
        grid=(2,),
        in_specs=[
            pl.BlockSpec((count, 1), lambda s: (0, 0)),
            pl.BlockSpec((chips, 1, 2, 2, part, width), lambda s: (0, s, 0, 0, 0, 0)),
        ],
        out_specs=[pl.BlockSpec((count, width), lambda s: (0, s))] * 2,
        out_shape=(out, out),
        name="order",
    )(tree_order[:, None], rows)


def per_device(mode_blocks, stiffness, mass_tiles, reader_ids, owner_slot, tile_mask, tree_order):
    devices = lax.axis_size("blk")
    count = lax.axis_size("sub") * devices
    place = lax.axis_index(AXES).astype(jnp.int32).reshape(1)
    swap = [(i, i ^ 1) for i in range(count)]

    def partner(x):
        return lax.ppermute(x, AXES, swap)

    def shift(x, chips):
        by = 2 * chips
        return lax.ppermute(x, AXES, [(i, i + by) for i in range(count) if 0 <= i + by < count])

    keep, send = pack(place, mode_blocks, TILE)
    pair = (keep, partner(send))
    held = []
    for chips in range(-(REACH // 2), REACH // 2 + 1):
        for x in pair:
            held.append(shift(x, -chips) if chips else x)
    ids = (reader_ids, partner(reader_ids))
    masks = (tile_mask, partner(tile_mask))
    stiff = (stiffness, partner(stiffness))
    mass = (mass_tiles, partner(mass_tiles))
    rows = project(place, owner_slot, ids, masks, stiff, mass, held, devices)
    rows = lax.all_to_all(rows, "blk", split_axis=0, concat_axis=0, tiled=True)
    return order_rows(tree_order, rows.reshape(devices // 2, 2, *rows.shape[1:]))


def solution(mesh):
    spec = P(AXES, None)
    return jax.shard_map(
        per_device,
        mesh=mesh,
        in_specs=(spec, spec, spec, spec, P(), spec, P(AXES)),
        out_specs=(spec, spec),
        check_vma=False,
    )
```

```python
import functools

import jax
import jax.numpy as jnp
from jax import lax
from jax.experimental import pallas as pl
from jax.experimental.pallas import tpu as pltpu
from jax.sharding import PartitionSpec as P

TILE = 128
REACH = 4
AXES = ("sub", "blk")
STEPS = 64.0
TOP = 32760.0
CODE_ROWS = 16
PACK_LIMIT = 60
VMEM = pl.BlockSpec(memory_space=pltpu.VMEM)


def quantize(x_ref, q_ref):
    tiles = x_ref.shape[0] // TILE
    codes = []
    for t in range(tiles):
        rows = pl.ds(t * TILE, TILE)
        x = x_ref[rows, :]
        top = jnp.maximum(jnp.max(jnp.abs(x), axis=0, keepdims=True), 2.0**-120)
        code = jnp.ceil(jnp.log2(top) * STEPS + 0.5)
        q = x * (jnp.exp2(code * (-1.0 / STEPS)) * TOP)
        q = jnp.minimum(jnp.maximum(q, -32767.0), 32767.0)
        q_ref[rows, :] = jnp.round(q).astype(jnp.int32).astype(jnp.int16)
        codes.append(code.astype(jnp.int32))
    codes.append(jnp.zeros((CODE_ROWS - tiles, x_ref.shape[1]), jnp.int32))
    q_ref[pl.ds(tiles * TILE, CODE_ROWS), :] = jnp.concatenate(codes, axis=0).astype(jnp.int16)


def pack_kernel(place_ref, *refs):
    for x_ref, q_ref in zip(refs[: len(refs) // 2], refs[len(refs) // 2 :], strict=True):
        quantize(x_ref, q_ref)


def pack(place, mode_blocks):
    rows, modes = mode_blocks.shape
    width = modes // 4
    steps = width // TILE
    out = jax.ShapeDtypeStruct((rows + CODE_ROWS, width), jnp.int16)

    def columns(piece):
        return lambda i, place: (0, (((place[0] + piece // 2) % 2) * 2 + piece % 2) * steps + i)

    return pl.pallas_call(
        pack_kernel,
        grid_spec=pltpu.PrefetchScalarGridSpec(
            num_scalar_prefetch=1,
            grid=(steps,),
            in_specs=[pl.BlockSpec((rows, TILE), columns(piece)) for piece in range(4)],
            out_specs=[pl.BlockSpec((rows + CODE_ROWS, TILE), lambda i, place: (0, i))] * 4,
        ),
        out_shape=(out,) * 4,
        compiler_params=pltpu.CompilerParams(vmem_limit_bytes=PACK_LIMIT << 20),
        cost_estimate=pl.CostEstimate(flops=rows * modes * 16, bytes_accessed=rows * modes * 6, transcendentals=0),
        name="pack",
    )(place, *[mode_blocks] * 4)


def slot_kernel(away, other, first, last, place_ref, owner_ref, own_ids, other_ids, own_mask, other_mask, *refs):
    own_rows, other_rows = refs[0:2], refs[2:4]
    a_ref, b_ref = refs[4:6]
    total = refs[6] if last or first else refs[7]
    high, low, left, landed = refs[-4:]
    outs = refs[7:-4]
    depth = high.shape[0]
    width = a_ref.shape[1]
    tiles = depth // TILE
    reads = own_ids.shape[1]
    index = place_ref[0]
    core = index % 2
    slot = index - core + 2 * away(index) + (core + other) % 2
    found, copies, at = [], [], []
    for who, (ids, rows) in enumerate(((own_ids, own_rows), (other_ids, other_rows))):
        read = jnp.int32(-1)
        for r in range(reads):
            read = jnp.where(owner_ref[ids[0, r]] == slot, jnp.int32(r), read)
        at.append(jnp.maximum(read, 0))
        span = pl.ds(pl.multiple_of(at[who] * depth, TILE), depth)
        height = rows[0].shape[0]
        copies.append(
            [
                pltpu.make_async_copy(x.at[:, span], left.at[who, pl.ds(kind * height, height)], landed.at[who, kind])
                for kind, x in enumerate(rows)
            ]
        )
        found.append(read >= 0)

        @pl.when(found[who])
        def _(who=who):
            for copy in copies[who]:
                copy.start()

    if first:
        total[...] = jnp.zeros_like(total)

    @pl.when(found[0] | found[1])
    def _():
        for piece, q_ref in enumerate((a_ref, b_ref)):
            columns = pl.ds(piece * width, width)
            codes = q_ref[pl.ds(depth, CODE_ROWS), :].astype(jnp.int32).astype(jnp.float32)
            scale = jnp.exp2(codes * (1.0 / STEPS)) * (1.0 / TOP)
            for t in range(tiles):
                span = pl.ds(t * TILE, TILE)
                value = q_ref[span, :].astype(jnp.int32).astype(jnp.float32) * scale[t : t + 1, :]
                top = value.astype(jnp.bfloat16)
                high[span, columns] = top
                low[span, columns] = (value - top.astype(jnp.float32)).astype(jnp.bfloat16)

    for who, mask in enumerate((own_mask, other_mask)):

        @pl.when(found[who])
        def _(who=who, mask=mask):
            for copy in copies[who]:
                copy.wait()
            row_tiles = mask.shape[0]
            for r in range(row_tiles):
                for t in range(tiles):

                    @pl.when(mask[r, at[who] * tiles + t] == 0)
                    def _(r=r, t=t):
                        for kind in range(2):
                            left[who, pl.ds((kind * row_tiles + r) * TILE, TILE), pl.ds(t * TILE, TILE)] = jnp.zeros(
                                (TILE, TILE), left.dtype
                            )

            step = 2 * TILE

            @pl.loop(0, high.shape[1] // step)
            def _(i):
                span = pl.ds(pl.multiple_of(i * step, step), step)
                total[who, :, span] += jnp.dot(left[who], high[:, span], preferred_element_type=jnp.float32) + jnp.dot(
                    left[who], low[:, span], preferred_element_type=jnp.float32
                )

    if last:
        _, kinds, part, _ = outs[0].shape
        for by, out_ref in enumerate(outs):
            for kind in range(kinds):
                to = index % len(outs) ^ by
                span = pl.ds(pl.multiple_of((kind * len(outs) + to) * part, part), part)
                for who in range(2):
                    out_ref[who, kind] = total[who, span, :].astype(jnp.bfloat16)
    else:
        refs[-5][...] = jnp.zeros_like(refs[-5])


def add_slot(place, away, other, owner_slot, ids, masks, rows, pieces, total, devices=None):
    height = rows[0][0].shape[0]
    depth = rows[0][0].shape[1] // ids[0].shape[1]
    width = 2 * pieces[0].shape[1]
    first, last = total is None, devices is not None
    if last:
        out_shape = [jax.ShapeDtypeStruct((2, 2, height // devices, width), jnp.bfloat16)] * devices
    else:
        out_shape = [jax.ShapeDtypeStruct((2, 2 * height, width), jnp.float32), jax.ShapeDtypeStruct((8, TILE), jnp.int32)]
    hbm = pl.BlockSpec(memory_space=pl.ANY)
    return pl.pallas_call(
        functools.partial(slot_kernel, away, other, first, last),
        grid_spec=pltpu.PrefetchScalarGridSpec(
            num_scalar_prefetch=6,
            grid=(),
            in_specs=[hbm] * 4 + [VMEM] * (2 if first else 3),
            out_specs=[VMEM] * len(out_shape),
            scratch_shapes=[
                pltpu.VMEM((depth, width), jnp.bfloat16),
                pltpu.VMEM((depth, width), jnp.bfloat16),
                pltpu.VMEM((2, 2 * height, depth), jnp.bfloat16),
                pltpu.SemaphoreType.DMA((2, 2)),
            ],
        ),
        out_shape=out_shape,
        input_output_aliases={} if first or last else {12: 0},
        compiler_params=pltpu.CompilerParams(vmem_limit_bytes=12 << 20),
        cost_estimate=pl.CostEstimate(flops=16 * height * depth * width, bytes_accessed=depth * width * 2, transcendentals=0),
        name="slot",
    )(place, owner_slot, *ids, *masks, *rows[0], *rows[1], *pieces, *(() if first else (total,)))


def order_kernel(place_ref, order_ref, *refs):
    outs, parts = refs[-2:], refs[:-2]
    _, _, part, width = parts[0].shape
    here = place_ref[0] % len(parts)
    count = order_ref.shape[0]
    at = lax.broadcasted_iota(jnp.int32, (count, count), 1)
    slot, who, row = at // (2 * part), at // part % 2, at % part
    for odd in range(2):
        core = (here + odd) % 2
        sender = here ^ (slot * 2 + odd)
        block = sender // 2 * 2 + (who + core) % 2
        pick = (order_ref[...] == block * part + row).astype(jnp.bfloat16)
        columns = pl.ds(pl.multiple_of(core * width, TILE), width)
        for kind, ref in enumerate(outs):
            if part % 16:
                rows = [x[who, kind].astype(jnp.float32) for x in parts[odd::2] for who in range(2)]
            else:
                rows = [x[who, kind] for x in parts[odd::2] for who in range(2)]
            rows = jnp.concatenate(rows, axis=0).astype(jnp.bfloat16)
            ref[:, columns] = jnp.dot(pick, rows, preferred_element_type=jnp.float32).astype(jnp.bfloat16)


def order_rows(place, tree_order, parts):
    count, width = tree_order.shape[0], parts[0].shape[-1]
    out = jax.ShapeDtypeStruct((count, 2 * width), jnp.bfloat16)
    return pl.pallas_call(
        order_kernel,
        grid_spec=pltpu.PrefetchScalarGridSpec(
            num_scalar_prefetch=1, grid=(), in_specs=[VMEM] * (1 + len(parts)), out_specs=[VMEM] * 2
        ),
        out_shape=(out, out),
        compiler_params=pltpu.CompilerParams(vmem_limit_bytes=12 << 20),
        name="order",
    )(place, tree_order[:, None], *parts)


def after(x, *landed):
    return lax.optimization_barrier((x, *landed))[0] if landed else x


def permute(x, count, target):
    pairs = [(i, target(i)) for i in range(count)]
    return lax.ppermute(x, AXES, [(i, t) for i, t in pairs if t is not None and 0 <= t < count])


def direct(own, partners, count, index, add):
    slots = [(lambda index: 0, own)]
    for chips in range(-(REACH // 2), REACH // 2 + 1):
        if chips:
            pieces = {k: permute(x, count, lambda i, by=-2 * chips: i + by) for k, x in own.items()}
            slots.append((lambda index, chips=chips: chips, pieces))
    for n, (away, pieces) in enumerate(slots):
        for other in range(2):
            parts = add(away, other, pieces, last=n == len(slots) - 1 and other == 1)
    return parts


def routed(own, partners, count, index, add):
    x, y, z, half, d = {}, {}, {}, {}, {}

    def beside(k, *landed):
        x[k] = permute(after(own[k], *landed), count, lambda i: i ^ 2)
        y[k] = permute(after(own[k], *landed), count, lambda i: i ^ 4)

    def beyond(k, *landed):
        z[k] = permute(after(y[k], *landed), count, lambda i: i - 8 if i & 4 else i + 8)
        if k[1] == 1:
            target = lambda i: None if (i >> 2 ^ i >> 1) & 1 == 0 else (i + 8 if i & 4 else i - 8)
            half[k] = permute(after(x[k], *landed), count, target)

    def around(k, *landed):
        outer = (index // 4 % 2) == (index // 2 % 2)
        if k[1] == 0:
            d[k] = permute(after(jnp.where(outer, y[k], z[k]), *landed), count, lambda i: i ^ 2)
        else:
            d[k] = permute(after(jnp.where(outer, x[k], half[k]), *landed), count, lambda i: i ^ 4)

    away = {
        "own": lambda index: 0,
        "x": lambda index: 1 - 2 * (index // 2 % 2),
        "y": lambda index: 2 - 4 * (index // 4 % 2),
        "z": lambda index: 4 * (index // 4 % 2) - 2,
        "d": lambda index: 2 * (index // 2 % 2) - 1,
    }
    oa, ob, pa, pb = (0, 0), (0, 1), (1, 0), (1, 1)
    beside(oa)
    beside(ob)
    beside(pa, x[oa], y[oa], *partners)
    beyond(oa)
    add(away["own"], 0, own, x[oa], y[oa])
    done = add(away["own"], 1, own)
    beside(pb, x[ob], y[ob], done)
    beyond(ob)
    add(away["x"], 0, x)
    done = add(away["y"], 0, y)
    around(oa)
    beyond(pa, done)
    around(ob)
    done = add(away["z"], 0, z)
    beyond(pb, done)
    add(away["x"], 1, x)
    done = add(away["y"], 1, y)
    around(pa, done)
    around(pb, done)
    add(away["z"], 1, z)
    add(away["d"], 0, d)
    return add(away["d"], 1, d, last=True)


def per_device(mode_blocks, stiffness, mass_tiles, reader_ids, owner_slot, tile_mask, tree_order):
    devices = lax.axis_size("blk")
    count = lax.axis_size("sub") * devices
    index = lax.axis_index(AXES).astype(jnp.int32)
    place = index.reshape(1)

    def partner(x):
        return permute(x, count, lambda i: i ^ 1)

    packed = pack(place, mode_blocks)
    keys = ((0, 0), (0, 1), (1, 0), (1, 1))
    own = dict(zip(keys, (*packed[:2], *(partner(x) for x in packed[2:])), strict=True))
    partners = [partner(x) for x in (stiffness, mass_tiles, reader_ids, tile_mask)]
    rows = ((stiffness, mass_tiles), tuple(partners[:2]))
    ids, masks = (reader_ids, partners[2]), (tile_mask, partners[3])
    total = [None]

    def add(away, other, pieces, *landed, last=False):
        pair = (pieces[other, 0], pieces[other, 1])
        out = add_slot(after(place, *landed), away, other, owner_slot, ids, masks, rows, pair, total[0], devices if last else None)
        if last:
            return out
        total[0], token = out
        return token

    parts = (routed if devices == 8 else direct)(own, partners, count, index, add)
    parts = [permute(x, count, lambda i, by=by: i ^ by) if by else x for by, x in enumerate(parts)]
    return order_rows(place, tree_order, parts)


def solution(mesh):
    spec = P(AXES, None)
    return jax.shard_map(
        per_device,
        mesh=mesh,
        in_specs=(spec, spec, spec, spec, P(), spec, P(AXES)),
        out_specs=(spec, spec),
        check_vma=False,
    )
```

```python
import functools

import jax
import jax.numpy as jnp
from jax import lax
from jax.experimental import pallas as pl
from jax.experimental.pallas import tpu as pltpu
from jax.sharding import PartitionSpec as P

TILE = 128
REACH = 4
AXES = ("sub", "blk")
STEPS = 64.0
TOP = 32760.0
CODE_ROWS = 16
VMEM = pl.BlockSpec(memory_space=pltpu.VMEM)


def quantize(x_ref, q_ref, columns):
    tiles = x_ref.shape[0] // TILE
    codes = []
    for t in range(tiles):
        rows = pl.ds(t * TILE, TILE)
        x = x_ref[rows, :]
        top = jnp.maximum(jnp.max(jnp.abs(x), axis=0, keepdims=True), 2.0**-120)
        code = jnp.ceil(jnp.log2(top) * STEPS + 0.5)
        q = x * (jnp.exp2(code * (-1.0 / STEPS)) * TOP)
        q = jnp.minimum(jnp.maximum(q, -32767.0), 32767.0)
        q_ref[rows, columns] = jnp.round(q).astype(jnp.int32).astype(jnp.int16)
        codes.append(code.astype(jnp.int32))
    codes.append(jnp.zeros((CODE_ROWS - tiles, x_ref.shape[1]), jnp.int32))
    q_ref[pl.ds(tiles * TILE, CODE_ROWS), columns] = jnp.concatenate(codes, axis=0).astype(jnp.int16)


def pack_kernel(pieces, place_ref, source, *refs):
    outs, (held, landed) = refs[-2 - len(pieces) : -2], refs[-2:]
    steps = outs[0].shape[1] // TILE
    copies = []
    for n, piece in enumerate(pieces):
        for i in range(steps):
            block = ((place_ref[0] + piece // 2) % 2 * 2 + piece % 2) * steps + i
            at = pl.multiple_of(block * TILE, TILE)
            k = n * steps + i
            copies.append(pltpu.make_async_copy(source.at[:, pl.ds(at, TILE)], held.at[k], landed.at[k]))
            copies[-1].start()
    for k, copy in enumerate(copies):
        copy.wait()
        quantize(held.at[k], outs[k // steps], pl.ds(k % steps * TILE, TILE))


def pack(place, mode_blocks, pieces, grant, *landed):
    rows, modes = mode_blocks.shape
    width = modes // 4
    tiles = len(pieces) * width // TILE
    return pl.pallas_call(
        functools.partial(pack_kernel, pieces),
        grid_spec=pltpu.PrefetchScalarGridSpec(
            num_scalar_prefetch=1,
            grid=(),
            in_specs=[pl.BlockSpec(memory_space=pltpu.HBM)] + [pl.BlockSpec(memory_space=pl.ANY)] * len(landed),
            out_specs=[VMEM] * len(pieces),
            scratch_shapes=[pltpu.VMEM((tiles, rows, TILE), jnp.float32), pltpu.SemaphoreType.DMA((tiles,))],
        ),
        out_shape=[jax.ShapeDtypeStruct((rows + CODE_ROWS, width), jnp.int16)] * len(pieces),
        compiler_params=pltpu.CompilerParams(vmem_limit_bytes=grant << 20),
        cost_estimate=pl.CostEstimate(
            flops=tiles * rows * TILE * 16, bytes_accessed=tiles * rows * TILE * 6, transcendentals=0
        ),
        name="pack",
    )(place, mode_blocks, *landed)


def slot_kernel(away, other, outs, first, last, place_ref, owner_ref, own_ids, other_ids, own_mask, other_mask, *refs):
    own_rows, other_rows = refs[0:2], refs[2:4]
    a_ref, b_ref = refs[4:6]
    high, low, left, landed = refs[-4:]
    outs = refs[-4 - outs :][:outs]
    total = refs[6] if last else outs[0]
    depth = high.shape[0]
    width = a_ref.shape[1]
    tiles = depth // TILE
    reads = own_ids.shape[1]
    index = place_ref[0]
    core = index % 2
    slot = index - core + 2 * away(index) + (core + other) % 2
    found, copies, at = [], [], []
    for who, (ids, rows) in enumerate(((own_ids, own_rows), (other_ids, other_rows))):
        read = jnp.int32(-1)
        for r in range(reads):
            read = jnp.where(owner_ref[ids[0, r]] == slot, jnp.int32(r), read)
        at.append(jnp.maximum(read, 0))
        span = pl.ds(pl.multiple_of(at[who] * depth, TILE), depth)
        height = rows[0].shape[0]
        copies.append(
            [
                pltpu.make_async_copy(x.at[:, span], left.at[who, pl.ds(kind * height, height)], landed.at[who, kind])
                for kind, x in enumerate(rows)
            ]
        )
        found.append(read >= 0)

        @pl.when(found[who])
        def _(who=who):
            for copy in copies[who]:
                copy.start()

    if first:
        total[...] = jnp.zeros_like(total)

    @pl.when(found[0] | found[1])
    def _():
        for piece, q_ref in enumerate((a_ref, b_ref)):
            columns = pl.ds(piece * width, width)
            codes = q_ref[pl.ds(depth, CODE_ROWS), :].astype(jnp.int32).astype(jnp.float32)
            scale = jnp.exp2(codes * (1.0 / STEPS)) * (1.0 / TOP)
            for t in range(tiles):
                span = pl.ds(t * TILE, TILE)
                value = q_ref[span, :].astype(jnp.int32).astype(jnp.float32) * scale[t : t + 1, :]
                top = value.astype(jnp.bfloat16)
                high[span, columns] = top
                low[span, columns] = (value - top.astype(jnp.float32)).astype(jnp.bfloat16)

    for who, mask in enumerate((own_mask, other_mask)):

        @pl.when(found[who])
        def _(who=who, mask=mask):
            for copy in copies[who]:
                copy.wait()
            row_tiles = mask.shape[0]
            for r in range(row_tiles):
                for t in range(tiles):

                    @pl.when(mask[r, at[who] * tiles + t] == 0)
                    def _(r=r, t=t):
                        for kind in range(2):
                            left[who, pl.ds((kind * row_tiles + r) * TILE, TILE), pl.ds(t * TILE, TILE)] = jnp.zeros(
                                (TILE, TILE), left.dtype
                            )

            total[who] += jnp.dot(left[who], high[...], preferred_element_type=jnp.float32) + jnp.dot(
                left[who], low[...], preferred_element_type=jnp.float32
            )

    if last:
        _, kinds, part, _ = outs[0].shape
        for by, out_ref in enumerate(outs):
            for kind in range(kinds):
                to = index % len(outs) ^ by
                span = pl.ds(pl.multiple_of((kind * len(outs) + to) * part, part), part)
                for who in range(2):
                    out_ref[who, kind] = total[who, span, :].astype(jnp.bfloat16)


def add_slot(place, away, other, owner_slot, ids, masks, rows, pieces, total, devices=None, hold=()):
    height = rows[0][0].shape[0]
    depth = rows[0][0].shape[1] // ids[0].shape[1]
    width = 2 * pieces[0].shape[1]
    first, last = total is None, devices is not None
    if last:
        out_shape = [jax.ShapeDtypeStruct((2, 2, height // devices, width), jnp.bfloat16)] * devices
    else:
        out_shape = [jax.ShapeDtypeStruct((2, 2 * height, width), jnp.float32)]
    sums = len(out_shape)
    out_shape += [jax.ShapeDtypeStruct(x.shape, x.dtype) for x in hold]
    anywhere = pl.BlockSpec(memory_space=pl.ANY)
    at = 12 if first else 13
    aliases = {at + n: sums + n for n in range(len(hold))}
    if not (first or last):
        aliases[12] = 0
    return pl.pallas_call(
        functools.partial(slot_kernel, away, other, len(out_shape), first, last),
        grid_spec=pltpu.PrefetchScalarGridSpec(
            num_scalar_prefetch=6,
            grid=(),
            in_specs=[pl.BlockSpec(memory_space=pltpu.HBM)] * 4 + [VMEM] * (2 if first else 3) + [anywhere] * len(hold),
            out_specs=[VMEM] * sums + [anywhere] * len(hold),
            scratch_shapes=[
                pltpu.VMEM((depth, width), jnp.bfloat16),
                pltpu.VMEM((depth, width), jnp.bfloat16),
                pltpu.VMEM((2, 2 * height, depth), jnp.bfloat16),
                pltpu.SemaphoreType.DMA((2, 2)),
            ],
        ),
        out_shape=out_shape,
        input_output_aliases=aliases,
        compiler_params=pltpu.CompilerParams(vmem_limit_bytes=44 << 20),
        cost_estimate=pl.CostEstimate(flops=4 * height * depth * width, bytes_accessed=depth * width // 2, transcendentals=0),
        name="slot",
    )(place, owner_slot, *ids, *masks, *rows[0], *rows[1], *pieces, *(() if first else (total,)), *hold)


def order_kernel(place_ref, order_ref, *refs):
    outs, parts = refs[-2:], refs[:-2]
    _, _, part, width = parts[0].shape
    here = place_ref[0] % len(parts)
    count = order_ref.shape[0]
    at = lax.broadcasted_iota(jnp.int32, (count, count), 1)
    slot, who, row = at // (2 * part), at // part % 2, at % part
    for odd in range(2):
        core = (here + odd) % 2
        sender = here ^ (slot * 2 + odd)
        block = sender // 2 * 2 + (who + core) % 2
        pick = (order_ref[...] == block * part + row).astype(jnp.bfloat16)
        columns = pl.ds(pl.multiple_of(core * width, TILE), width)
        for kind, ref in enumerate(outs):
            if part % 16:
                rows = [x[who, kind].astype(jnp.float32) for x in parts[odd::2] for who in range(2)]
            else:
                rows = [x[who, kind] for x in parts[odd::2] for who in range(2)]
            rows = jnp.concatenate(rows, axis=0).astype(jnp.bfloat16)
            ref[:, columns] = jnp.dot(pick, rows, preferred_element_type=jnp.float32).astype(jnp.bfloat16)


def order_rows(place, tree_order, parts):
    count, width = tree_order.shape[0], parts[0].shape[-1]
    out = jax.ShapeDtypeStruct((count, 2 * width), jnp.bfloat16)
    return pl.pallas_call(
        order_kernel,
        grid_spec=pltpu.PrefetchScalarGridSpec(
            num_scalar_prefetch=1, grid=(), in_specs=[VMEM] * (1 + len(parts)), out_specs=[VMEM] * 2
        ),
        out_shape=(out, out),
        compiler_params=pltpu.CompilerParams(vmem_limit_bytes=12 << 20),
        name="order",
    )(place, tree_order[:, None], *parts)


def after(x, *landed):
    return lax.optimization_barrier((x, *landed))[0] if landed else x


def permute(x, count, target):
    pairs = [(i, target(i)) for i in range(count)]
    return lax.ppermute(x, AXES, [(i, t) for i, t in pairs if t is not None and 0 <= t < count])


def direct(own, count, index, add):
    slots = [(lambda index: 0, own)]
    for chips in range(-(REACH // 2), REACH // 2 + 1):
        if chips:
            pieces = {k: permute(x, count, lambda i, by=-2 * chips: i + by) for k, x in own.items()}
            slots.append((lambda index, chips=chips: chips, pieces))
    for n, (away, pieces) in enumerate(slots):
        for other in range(2):
            parts = add(away, other, pieces, last=n == len(slots) - 1 and other == 1)
    return parts


def routed(own, count, index, add):
    x, y, z, half, d = {}, {}, {}, {}, {}
    outer = (index // 4 % 2) == (index // 2 % 2)

    def beside(k, *landed):
        x[k] = permute(after(own[k], *landed), count, lambda i: i ^ 2)
        y[k] = permute(after(own[k], *landed), count, lambda i: i ^ 4)

    def beyond(k, *landed):
        z[k] = permute(after(y[k], *landed), count, lambda i: i - 8 if i & 4 else i + 8)

    def beyond_half(k, *landed):
        target = lambda i: None if (i >> 2 ^ i >> 1) & 1 == 0 else (i + 8 if i & 4 else i - 8)
        half[k] = permute(after(x[k], *landed), count, target)

    def around(k):
        return jnp.where(outer, x[k], half[k]) if k[1] else jnp.where(outer, y[k], z[k])

    away = {
        "own": lambda index: 0,
        "x": lambda index: 1 - 2 * (index // 2 % 2),
        "y": lambda index: 2 - 4 * (index // 4 % 2),
        "z": lambda index: 4 * (index // 4 % 2) - 2,
        "d": lambda index: 2 * (index // 2 % 2) - 1,
    }
    oa, ob, pa, pb = (0, 0), (0, 1), (1, 0), (1, 1)
    beside(oa)
    beside(ob)
    beside(pa, x[oa], y[oa], own[pb])
    beyond(oa)
    (own[pb],) = add(away["own"], 0, own, hold=(own[pb],))
    add(away["own"], 1, own)
    beside(pb, x[ob], y[ob])
    beyond(ob, z[oa])
    add(away["x"], 0, x)
    (passed,) = add(away["y"], 0, y, hold=(around(oa),))
    beyond_half(ob, x[pa], z[oa])
    beyond(pa)
    d[oa] = permute(after(passed, z[ob]), count, lambda i: i ^ 2)
    add(away["z"], 0, z)
    d[ob] = permute(around(ob), count, lambda i: i ^ 4)
    beyond_half(pb)
    beyond(pb)
    (passed,) = add(away["x"], 1, x, hold=(around(pa),))
    d[pa] = permute(passed, count, lambda i: i ^ 2)
    add(away["y"], 1, y)
    d[pb] = permute(around(pb), count, lambda i: i ^ 4)
    add(away["z"], 1, z)
    add(away["d"], 0, d)
    return add(away["d"], 1, d, last=True)


def per_device(mode_blocks, stiffness, mass_tiles, reader_ids, owner_slot, tile_mask, tree_order):
    devices = lax.axis_size("blk")
    count = lax.axis_size("sub") * devices
    index = lax.axis_index(AXES).astype(jnp.int32)
    place = index.reshape(1)

    def partner(x):
        return permute(x, count, lambda i: i ^ 1)

    partners = [partner(x) for x in (stiffness, mass_tiles)]
    partners += [partner(after(x, *partners)) for x in (reader_ids, tile_mask)]
    (first,) = pack(place, mode_blocks, (0,), 60)
    second, *sent = pack(place, mode_blocks, (1, 2, 3), 48, *partners[:2], first)
    own = dict(zip(((0, 0), (0, 1), (1, 0), (1, 1)), (first, second, *map(partner, sent)), strict=True))
    rows = ((stiffness, mass_tiles), tuple(partners[:2]))
    ids, masks = (reader_ids, partners[2]), (tile_mask, partners[3])
    total = [None]

    def add(away, other, pieces, last=False, hold=()):
        pair = (pieces[other, 0], pieces[other, 1])
        out = add_slot(place, away, other, owner_slot, ids, masks, rows, pair, total[0], devices if last else None, hold)
        if last:
            return out
        total[0] = out[0]
        return out[1:]

    parts = (routed if devices == 8 else direct)(own, count, index, add)
    parts = [permute(x, count, lambda i, by=by: i ^ by) if by else x for by, x in enumerate(parts)]
    return order_rows(place, tree_order, parts)


def solution(mesh):
    spec = P(AXES, None)
    return jax.shard_map(
        per_device,
        mesh=mesh,
        in_specs=(spec, spec, spec, spec, P(), spec, P(AXES)),
        out_specs=(spec, spec),
        check_vma=False,
    )
```

```python
import functools

import jax
import jax.numpy as jnp
from jax import lax
from jax.experimental import pallas as pl
from jax.experimental.pallas import tpu as pltpu
from jax.sharding import PartitionSpec as P

TILE = 128
REACH = 4
AXES = ("sub", "blk")
STEPS = 64.0
TOP = 32760.0
CODE_ROWS = 16
VMEM = pl.BlockSpec(memory_space=pltpu.VMEM)


def quantize(x_ref, q_ref, columns):
    tiles = x_ref.shape[0] // TILE
    codes = []
    for t in range(tiles):
        rows = pl.ds(t * TILE, TILE)
        x = x_ref[rows, :]
        top = jnp.maximum(jnp.max(jnp.abs(x), axis=0, keepdims=True), 2.0**-120)
        code = jnp.ceil(jnp.log2(top) * STEPS + 0.5)
        q = x * (jnp.exp2(code * (-1.0 / STEPS)) * TOP)
        q = jnp.minimum(jnp.maximum(q, -32767.0), 32767.0)
        q_ref[rows, columns] = jnp.round(q).astype(jnp.int32).astype(jnp.int16)
        codes.append(code.astype(jnp.int32))
    codes.append(jnp.zeros((CODE_ROWS - tiles, x_ref.shape[1]), jnp.int32))
    q_ref[pl.ds(tiles * TILE, CODE_ROWS), columns] = jnp.concatenate(codes, axis=0).astype(jnp.int16)


def pack_kernel(pieces, place_ref, source, *refs):
    outs, (held, landed) = refs[-2 - len(pieces) : -2], refs[-2:]
    steps = outs[0].shape[1] // TILE
    copies = []
    for n, piece in enumerate(pieces):
        for i in range(steps):
            block = ((place_ref[0] + piece // 2) % 2 * 2 + piece % 2) * steps + i
            at = pl.multiple_of(block * TILE, TILE)
            k = n * steps + i
            copies.append(pltpu.make_async_copy(source.at[:, pl.ds(at, TILE)], held.at[k], landed.at[k]))
            copies[-1].start()
    for k, copy in enumerate(copies):
        copy.wait()
        quantize(held.at[k], outs[k // steps], pl.ds(k % steps * TILE, TILE))


def pack(place, mode_blocks, pieces, grant, *landed):
    rows, modes = mode_blocks.shape
    width = modes // 4
    tiles = len(pieces) * width // TILE
    return pl.pallas_call(
        functools.partial(pack_kernel, pieces),
        grid_spec=pltpu.PrefetchScalarGridSpec(
            num_scalar_prefetch=1,
            grid=(),
            in_specs=[pl.BlockSpec(memory_space=pltpu.HBM)] + [pl.BlockSpec(memory_space=pl.ANY)] * len(landed),
            out_specs=[VMEM] * len(pieces),
            scratch_shapes=[pltpu.VMEM((tiles, rows, TILE), jnp.float32), pltpu.SemaphoreType.DMA((tiles,))],
        ),
        out_shape=[jax.ShapeDtypeStruct((rows + CODE_ROWS, width), jnp.int16)] * len(pieces),
        compiler_params=pltpu.CompilerParams(vmem_limit_bytes=grant << 20),
        cost_estimate=pl.CostEstimate(
            flops=tiles * rows * TILE * 16, bytes_accessed=tiles * rows * TILE * 6, transcendentals=0
        ),
        name="pack",
    )(place, mode_blocks, *landed)


def slot_kernel(away, other, outs, first, last, place_ref, owner_ref, own_ids, other_ids, own_mask, other_mask, *refs):
    own_rows, other_rows = refs[0:2], refs[2:4]
    a_ref, b_ref = refs[4:6]
    high, low, left, landed = refs[-4:]
    outs = refs[-4 - outs :][:outs]
    total = refs[6] if last else outs[0]
    depth = high.shape[0]
    width = a_ref.shape[1]
    tiles = depth // TILE
    reads = own_ids.shape[1]
    index = place_ref[0]
    core = index % 2
    slot = index - core + 2 * away(index) + (core + other) % 2
    found, copies, at = [], [], []
    for who, (ids, rows) in enumerate(((own_ids, own_rows), (other_ids, other_rows))):
        read = jnp.int32(-1)
        for r in range(reads):
            read = jnp.where(owner_ref[ids[0, r]] == slot, jnp.int32(r), read)
        at.append(jnp.maximum(read, 0))
        span = pl.ds(pl.multiple_of(at[who] * depth, TILE), depth)
        height = rows[0].shape[0]
        copies.append(
            [
                pltpu.make_async_copy(x.at[:, span], left.at[who, pl.ds(kind * height, height)], landed.at[who, kind])
                for kind, x in enumerate(rows)
            ]
        )
        found.append(read >= 0)

        @pl.when(found[who])
        def _(who=who):
            for copy in copies[who]:
                copy.start()

    if first:
        total[...] = jnp.zeros_like(total)

    @pl.when(found[0] | found[1])
    def _():
        for piece, q_ref in enumerate((a_ref, b_ref)):
            columns = pl.ds(piece * width, width)
            codes = q_ref[pl.ds(depth, CODE_ROWS), :].astype(jnp.int32).astype(jnp.float32)
            scale = jnp.exp2(codes * (1.0 / STEPS)) * (1.0 / TOP)
            for t in range(tiles):
                span = pl.ds(t * TILE, TILE)
                value = q_ref[span, :].astype(jnp.int32).astype(jnp.float32) * scale[t : t + 1, :]
                top = value.astype(jnp.bfloat16)
                high[span, columns] = top
                low[span, columns] = (value - top.astype(jnp.float32)).astype(jnp.bfloat16)

    for who, mask in enumerate((own_mask, other_mask)):

        @pl.when(found[who])
        def _(who=who, mask=mask):
            for copy in copies[who]:
                copy.wait()
            row_tiles = mask.shape[0]
            for r in range(row_tiles):
                for t in range(tiles):

                    @pl.when(mask[r, at[who] * tiles + t] == 0)
                    def _(r=r, t=t):
                        for kind in range(2):
                            left[who, pl.ds((kind * row_tiles + r) * TILE, TILE), pl.ds(t * TILE, TILE)] = jnp.zeros(
                                (TILE, TILE), left.dtype
                            )

            total[who] += jnp.dot(left[who], high[...], preferred_element_type=jnp.float32) + jnp.dot(
                left[who], low[...], preferred_element_type=jnp.float32
            )

    if last:
        _, kinds, part, _ = outs[0].shape
        for by, out_ref in enumerate(outs):
            for kind in range(kinds):
                to = index % len(outs) ^ by
                span = pl.ds(pl.multiple_of((kind * len(outs) + to) * part, part), part)
                for who in range(2):
                    out_ref[who, kind] = total[who, span, :].astype(jnp.bfloat16)


def add_slot(place, away, other, owner_slot, ids, masks, rows, pieces, total, devices=None, hold=()):
    height = rows[0][0].shape[0]
    depth = rows[0][0].shape[1] // ids[0].shape[1]
    width = 2 * pieces[0].shape[1]
    first, last = total is None, devices is not None
    if last:
        out_shape = [jax.ShapeDtypeStruct((2, 2, height // devices, width), jnp.bfloat16)] * devices
    else:
        out_shape = [jax.ShapeDtypeStruct((2, 2 * height, width), jnp.float32)]
    sums = len(out_shape)
    out_shape += [jax.ShapeDtypeStruct(x.shape, x.dtype) for x in hold]
    anywhere = pl.BlockSpec(memory_space=pl.ANY)
    at = 12 if first else 13
    aliases = {at + n: sums + n for n in range(len(hold))}
    if not (first or last):
        aliases[12] = 0
    return pl.pallas_call(
        functools.partial(slot_kernel, away, other, len(out_shape), first, last),
        grid_spec=pltpu.PrefetchScalarGridSpec(
            num_scalar_prefetch=6,
            grid=(),
            in_specs=[pl.BlockSpec(memory_space=pltpu.HBM)] * 4 + [VMEM] * (2 if first else 3) + [anywhere] * len(hold),
            out_specs=[VMEM] * sums + [anywhere] * len(hold),
            scratch_shapes=[
                pltpu.VMEM((depth, width), jnp.bfloat16),
                pltpu.VMEM((depth, width), jnp.bfloat16),
                pltpu.VMEM((2, 2 * height, depth), jnp.bfloat16),
                pltpu.SemaphoreType.DMA((2, 2)),
            ],
        ),
        out_shape=out_shape,
        input_output_aliases=aliases,
        compiler_params=pltpu.CompilerParams(vmem_limit_bytes=44 << 20),
        cost_estimate=pl.CostEstimate(flops=4 * height * depth * width, bytes_accessed=depth * width // 2, transcendentals=0),
        name="slot",
    )(place, owner_slot, *ids, *masks, *rows[0], *rows[1], *pieces, *(() if first else (total,)), *hold)


def order_kernel(place_ref, order_ref, *refs):
    outs, parts = refs[-2:], refs[:-2]
    _, _, part, width = parts[0].shape
    here = place_ref[0] % len(parts)
    count = order_ref.shape[0]
    at = lax.broadcasted_iota(jnp.int32, (count, count), 1)
    slot, who, row = at // (2 * part), at // part % 2, at % part
    for odd in range(2):
        core = (here + odd) % 2
        sender = here ^ (slot * 2 + odd)
        block = sender // 2 * 2 + (who + core) % 2
        pick = (order_ref[...] == block * part + row).astype(jnp.bfloat16)
        columns = pl.ds(pl.multiple_of(core * width, TILE), width)
        for kind, ref in enumerate(outs):
            if part % 16:
                rows = [x[who, kind].astype(jnp.float32) for x in parts[odd::2] for who in range(2)]
            else:
                rows = [x[who, kind] for x in parts[odd::2] for who in range(2)]
            rows = jnp.concatenate(rows, axis=0).astype(jnp.bfloat16)
            ref[:, columns] = jnp.dot(pick, rows, preferred_element_type=jnp.float32).astype(jnp.bfloat16)


def order_rows(place, tree_order, parts):
    count, width = tree_order.shape[0], parts[0].shape[-1]
    out = jax.ShapeDtypeStruct((count, 2 * width), jnp.bfloat16)
    return pl.pallas_call(
        order_kernel,
        grid_spec=pltpu.PrefetchScalarGridSpec(
            num_scalar_prefetch=1, grid=(), in_specs=[VMEM] * (1 + len(parts)), out_specs=[VMEM] * 2
        ),
        out_shape=(out, out),
        compiler_params=pltpu.CompilerParams(vmem_limit_bytes=12 << 20),
        name="order",
    )(place, tree_order[:, None], *parts)


def after(x, *landed):
    return lax.optimization_barrier((x, *landed))[0] if landed else x


def permute(x, count, target):
    pairs = [(i, target(i)) for i in range(count)]
    return lax.ppermute(x, AXES, [(i, t) for i, t in pairs if t is not None and 0 <= t < count])


def direct(own, count, index, add):
    slots = [(lambda index: 0, own)]
    for chips in range(-(REACH // 2), REACH // 2 + 1):
        if chips:
            pieces = {k: permute(x, count, lambda i, by=-2 * chips: i + by) for k, x in own.items()}
            slots.append((lambda index, chips=chips: chips, pieces))
    for n, (away, pieces) in enumerate(slots):
        for other in range(2):
            parts = add(away, other, pieces, last=n == len(slots) - 1 and other == 1)
    return parts


def routed(own, count, index, add):
    x, y, z, half, d = {}, {}, {}, {}, {}
    outer = (index // 4 % 2) == (index // 2 % 2)

    def beside(k, *landed):
        x[k] = permute(after(own[k], *landed), count, lambda i: i ^ 2)
        y[k] = permute(after(own[k], *landed), count, lambda i: i ^ 4)

    def beyond(k, *landed):
        z[k] = permute(after(y[k], *landed), count, lambda i: i - 8 if i & 4 else i + 8)

    def beyond_half(k, *landed):
        target = lambda i: None if (i >> 2 ^ i >> 1) & 1 == 0 else (i + 8 if i & 4 else i - 8)
        half[k] = permute(after(x[k], *landed), count, target)

    def around(k):
        return jnp.where(outer, x[k], half[k]) if k[1] else jnp.where(outer, y[k], z[k])

    away = {
        "own": lambda index: 0,
        "x": lambda index: 1 - 2 * (index // 2 % 2),
        "y": lambda index: 2 - 4 * (index // 4 % 2),
        "z": lambda index: 4 * (index // 4 % 2) - 2,
        "d": lambda index: 2 * (index // 2 % 2) - 1,
    }
    oa, ob, pa, pb = (0, 0), (0, 1), (1, 0), (1, 1)
    beside(oa)
    beside(ob)
    beside(pa, x[oa], y[oa], own[pb])
    beyond(oa)
    (own[pb],) = add(away["own"], 0, own, hold=(own[pb],))
    add(away["own"], 1, own)
    beside(pb, x[ob], y[ob])
    beyond(ob, z[oa])
    add(away["x"], 0, x)
    (passed,) = add(away["y"], 0, y, hold=(around(oa),))
    beyond_half(ob, x[pa], z[oa])
    beyond(pa)
    d[oa] = permute(after(passed, z[ob]), count, lambda i: i ^ 2)
    add(away["z"], 0, z)
    d[ob] = permute(around(ob), count, lambda i: i ^ 4)
    beyond_half(pb)
    beyond(pb)
    (passed,) = add(away["x"], 1, x, hold=(around(pa),))
    d[pa] = permute(passed, count, lambda i: i ^ 2)
    add(away["y"], 1, y)
    d[pb] = permute(around(pb), count, lambda i: i ^ 4)
    add(away["z"], 1, z)
    add(away["d"], 0, d)
    return add(away["d"], 1, d, last=True)


def per_device(mode_blocks, stiffness, mass_tiles, reader_ids, owner_slot, tile_mask, tree_order):
    devices = lax.axis_size("blk")
    count = lax.axis_size("sub") * devices
    index = lax.axis_index(AXES).astype(jnp.int32)
    place = index.reshape(1)

    def partner(x):
        return permute(x, count, lambda i: i ^ 1)

    partners = [partner(x) for x in (stiffness, mass_tiles)]
    partners += [partner(after(x, *partners)) for x in (reader_ids, tile_mask)]
    (first,) = pack(place, mode_blocks, (0,), 60)
    second, *sent = pack(place, mode_blocks, (1, 2, 3), 48, *partners[:2], first)
    own = dict(zip(((0, 0), (0, 1), (1, 0), (1, 1)), (first, second, *map(partner, sent)), strict=True))
    rows = ((stiffness, mass_tiles), tuple(partners[:2]))
    ids, masks = (reader_ids, partners[2]), (tile_mask, partners[3])
    total = [None]

    def add(away, other, pieces, last=False, hold=()):
        pair = (pieces[other, 0], pieces[other, 1])
        out = add_slot(place, away, other, owner_slot, ids, masks, rows, pair, total[0], devices if last else None, hold)
        if last:
            return out
        total[0] = out[0]
        return out[1:]

    parts = (routed if devices == 8 else direct)(own, count, index, add)
    parts = list(parts)
    for by in sorted(range(1, devices), key=lambda by: (-bin(by >> 1).count("1"), -by)):
        parts[by] = permute(parts[by], count, lambda i, by=by: i ^ by)
    return order_rows(place, tree_order, parts)


def solution(mesh):
    spec = P(AXES, None)
    return jax.shard_map(
        per_device,
        mesh=mesh,
        in_specs=(spec, spec, spec, spec, P(), spec, P(AXES)),
        out_specs=(spec, spec),
        check_vma=False,
    )
```
